32 devices in a mesh: section: 2 (over x), batch: 16 (over z, y, core).
Axes of the slice: x: 2, y: 2, z: 4, core: 2. Of those that a mesh axis runs over, the one named last changes fastest.
Arguments:
- clips: bfloat16 [32, 512, 768], P('batch'), may hold values from -30 to 30
- mask_flags: int32 [32, 512], P('batch'), may hold values from 0 to 1, as said below
- mask_embed: float32 [768], replicated, may hold values from -4 to 4
- pos_embed: float32 [512, 768], replicated, may hold values from -2.5 to 2.5
- first_gain: float32 [2, 768], P('section'), may hold values from 0.25 to 1.75
- first_shift: float32 [2, 768], P('section'), may hold values from -1.5 to 1.5
- joint_weight: bfloat16 [2, 768, 2304], P('section'), may hold values from -0.21875 to 0.21875
- query_bias: float32 [2, 768], P('section'), may hold values from -2.5 to 2.5
- value_bias: float32 [2, 768], P('section'), may hold values from -2.5 to 2.5
- mixer_weight: bfloat16 [2, 768, 768], P('section'), may hold values from -2.5 to 2.5
- mixer_bias: float32 [2, 768], P('section'), may hold values from -1.5 to 1.5
- second_gain: float32 [2, 768], P('section'), may hold values from 0.25 to 1.75
- second_shift: float32 [2, 768], P('section'), may hold values from -1.5 to 1.5
- up_weight: bfloat16 [2, 768, 3072], P('section'), may hold values from -0.21875 to 0.21875
- up_bias: float32 [2, 3072], P('section'), may hold values from -2.5 to 2.5
- down_weight: bfloat16 [2, 3072, 768], P('section'), may hold values from -0.109375 to 0.109375
- down_bias: float32 [2, 768], P('section'), may hold values from -1.5 to 1.5
- out_grad: bfloat16 [32, 512, 768], P('batch'), may hold values from -6 to 6
Outputs:
- layer_outputs: bfloat16 [2, 32, 512, 768], P('section', 'batch')
- input_grads: bfloat16 [2, 32, 512, 768], P('section', 'batch')
- grad_first_gain: float32 [2, 768], P('section', 'batch')
- grad_first_shift: float32 [2, 768], P('section', 'batch')
- grad_joint_weight: float32 [2, 768, 2304], P('section', 'batch')
- grad_query_bias: float32 [2, 768], P('section', 'batch')
- grad_value_bias: float32 [2, 768], P('section', 'batch')
- grad_mixer_weight: float32 [2, 768, 768], P('section', 'batch')
- grad_mixer_bias: float32 [2, 768], P('section', 'batch')
- grad_second_gain: float32 [2, 768], P('section', 'batch')
- grad_second_shift: float32 [2, 768], P('section', 'batch')
- grad_up_weight: float32 [2, 768, 3072], P('section', 'batch')
- grad_up_bias: float32 [2, 3072], P('section', 'batch')
- grad_down_weight: float32 [2, 3072, 768], P('section', 'batch')
- grad_down_bias: float32 [2, 768], P('section', 'batch')
- grad_mask_embed: float32 [768], P('section')
- grad_pos_embed: float32 [512, 768], P('section')
The draws below stay inside these ranges and needn't reach their ends.
Inputs may be any that keep to these rules, and one draw needn't show every extreme that they name: `mask_flags`: every clip has exactly 400 patches set to 1.
All inputs are finite; a program needn't handle non-finite values.
Results may differ from the reference program's by a relative error of at most 0.012.
Values may be sent and summed in bfloat16 or wider, within the bound.
No kernel may reach another device: no remote copies, remote signals or barrier semaphores. Data moves between devices by JAX's collectives and lax.ppermute only.
A program may use at most 448 MiB of HBM per device.

```python
import math
import jax
import jax.numpy as jnp
from jax import lax

D = 768
HEADS = 12
HD = 64
FF = 3072
L = 512
MASKED = 400
CLIPS = 32


def draw_clips(key, part):
    base_key, row_key, column_key = jax.random.split(key, 3)
    base = jnp.clip(jax.random.normal(base_key, (CLIPS, L, D), jnp.float32), -5.0, 5.0)
    row_scale = jnp.exp(jax.random.uniform(row_key, (CLIPS, L, 1), jnp.float32, math.log(0.3), math.log(3.0)))
    column_scale = jnp.exp(jax.random.uniform(column_key, (1, 1, D), jnp.float32, math.log(0.5), math.log(2.0)))
    return (base * row_scale * column_scale).astype(jnp.bfloat16)


def draw_mask_flags(key, part):
    clip_keys = jax.random.split(key, CLIPS)
    orders = jax.vmap(lambda single: jax.random.permutation(single, L))(clip_keys)
    return (orders < MASKED).astype(jnp.int32)


def block_levels(stream_key, shape, shards, low, high):
    loudness, own = 1.0, jax.random.fold_in(stream_key, 6)
    for dim, parts in shards:
        heights = jnp.exp(jax.random.uniform(jax.random.fold_in(own, dim), (parts,), jnp.float32, low / len(shards), high / len(shards)))
        loudness = loudness * jnp.repeat(heights, shape[dim] // parts).reshape([-1 if axis == dim else 1 for axis in range(len(shape))])
    return loudness


def scatter_about(own_key, extent, deviation, limit, shards=(), dtype=jnp.bfloat16):
    result = jax.random.normal(own_key, extent, jnp.float32) * deviation
    if len(shards) > 0:
        result = block_levels(own_key, extent, shards, -0.22, 0.18) * result
    return jnp.clip(result, min=-limit, max=limit).astype(dtype)


def setup_inputs(seed: int = 0) -> dict:
    seeds = jax.random.split(jax.random.key(seed), 19)
    return {
        "clips": draw_clips(jax.random.fold_in(seeds[18], 71), 0),
        "mask_flags": draw_mask_flags(jax.random.fold_in(seeds[18], 71), 0),
        "mask_embed": scatter_about(seeds[2], (D,), 1.0, 4.0, (), jnp.float32),
        "pos_embed": scatter_about(seeds[3], (L, D), 0.5, 2.5, (), jnp.float32),
        "first_gain": jnp.clip(1.0 + 0.15 * jax.random.normal(seeds[4], (2, D), jnp.float32), 0.25, 1.75),
        "first_shift": scatter_about(seeds[5], (2, D), 0.3, 1.5, ((0, 2),), jnp.float32),
        "joint_weight": scatter_about(seeds[6], (2, D, 3 * D), D ** -0.5, 0.21875, ((0, 2),)),
        "query_bias": scatter_about(seeds[7], (2, D), 0.5, 2.5, ((0, 2),), jnp.float32),
        "value_bias": scatter_about(seeds[8], (2, D), 0.5, 2.5, ((0, 2),), jnp.float32),
        "mixer_weight": scatter_about(seeds[9], (2, D, D), (max(D * 4 // L, 1)) ** -0.5, 2.5, ((0, 2),)),
        "mixer_bias": scatter_about(seeds[10], (2, D), 0.3, 1.5, ((0, 2),), jnp.float32),
        "second_gain": jnp.clip(1.0 + 0.15 * jax.random.normal(seeds[11], (2, D), jnp.float32), 0.25, 1.75),
        "second_shift": scatter_about(seeds[12], (2, D), 0.3, 1.5, ((0, 2),), jnp.float32),
        "up_weight": scatter_about(seeds[13], (2, D, FF), D ** -0.5, 0.21875, ((0, 2),)),
        "up_bias": scatter_about(seeds[14], (2, FF), 0.5, 2.5, ((0, 2),), jnp.float32),
        "down_weight": scatter_about(seeds[15], (2, FF, D), FF ** -0.5, 0.109375, ((0, 2),)),
        "down_bias": scatter_about(seeds[16], (2, D), 0.3, 1.5, ((0, 2),), jnp.float32),
        "out_grad": scatter_about(seeds[17], (CLIPS, L, D), 1.0, 6.0, ((0, 16),)),
    }


highest = lax.Precision.HIGHEST

@jax.custom_vjp
def low(v):
    return lax.optimization_barrier(v.astype(jnp.bfloat16)).astype(jnp.float32)

@jax.custom_vjp
def low_back(v):
    return v

def low_keep(v):
    return (low(v), None)

def low_pass(kept, grad):
    return (grad,)

def back_keep(v):
    return (v, None)

def back_low(kept, grad):
    return (low(grad),)
low.defvjp(low_keep, low_pass)
low_back.defvjp(back_keep, back_low)

def norm_rows(value, gain, shift):
    average = lax.optimization_barrier(jnp.mean(value, axis=-1, keepdims=True))
    centered = value - average
    variance = lax.optimization_barrier(jnp.mean(centered * centered, axis=-1, keepdims=True))
    return centered * lax.rsqrt(variance + 1e-06) * gain + shift

def project(left, right):
    return jnp.einsum('gld,de->gle', left, right, precision=highest)

def block_forward(hidden, params):
    first_gain, first_shift, joint_weight, query_bias, value_bias, mixer_weight, mixer_bias, second_gain, second_shift, up_weight, up_bias, down_weight, down_bias = params
    groups = hidden.shape[0]
    normed = low(norm_rows(hidden, first_gain, first_shift))
    joint = project(normed, joint_weight)
    query = low_back(low(joint[..., :D] + query_bias))
    keys = low_back(low(joint[..., D:2 * D]))
    values = low_back(low(joint[..., 2 * D:] + value_bias))
    head_shape = (groups, L, HEADS, HD)
    scores = jnp.einsum('gqhc,gkhc->ghqk', query.reshape(head_shape), keys.reshape(head_shape), precision=highest)
    scores = low_back(scores * HD ** (-0.5))
    attention = low(jax.nn.softmax(scores, axis=-1))
    mixed = jnp.einsum('ghqk,gkhc->gqhc', attention, values.reshape(head_shape), precision=highest)
    mixed = low_back(low(mixed.reshape(groups, L, D)))
    after = hidden + low_back(project(mixed, mixer_weight) + mixer_bias)
    normed_second = low(norm_rows(after, second_gain, second_shift))
    lifted = low_back(project(normed_second, up_weight) + up_bias)
    active = low(jax.nn.gelu(lifted, approximate=False))
    return after + low_back(project(active, down_weight) + down_bias)

def reference(clips, mask_flags, mask_embed, pos_embed, first_gain, first_shift, joint_weight, query_bias, value_bias, mixer_weight, mixer_bias, second_gain, second_shift, up_weight, up_bias, down_weight, down_bias, out_grad):
    stacked = (first_gain, first_shift, joint_weight, query_bias, value_bias, mixer_weight, mixer_bias, second_gain, second_shift, up_weight, up_bias, down_weight, down_bias)
    params_one = tuple((weight[0].astype(jnp.float32) for weight in stacked))
    params_two = tuple((weight[1].astype(jnp.float32) for weight in stacked))
    keep = mask_flags.astype(jnp.float32)[..., None]
    group = math.gcd(CLIPS, max(1, 4096 // L))
    count = CLIPS // group

    def forward(inputs, embed, position, first, second, probe):
        blended = inputs * (1.0 - keep) + keep * embed + position

        def one_group(pair):
            block, extra = pair
            middle = low_back(low(block_forward(block, first)))
            final = block_forward(middle + extra, second)
            return (middle, final)
        middle, final = lax.map(jax.checkpoint(one_group), (blended.reshape(count, group, L, D), probe.reshape(count, group, L, D)))
        return (middle.reshape(CLIPS, L, D), final.reshape(CLIPS, L, D))
    probe = jnp.zeros((CLIPS, L, D), jnp.float32)
    (middle, final), pullback = jax.vjp(forward, clips.astype(jnp.float32), mask_embed, pos_embed, params_one, params_two, probe)
    cotangent = (jnp.zeros_like(middle), out_grad.astype(jnp.float32))
    grad_clips, grad_embed, grad_position, grads_one, grads_two, grad_probe = pullback(cotangent)
    layer_outputs = jnp.stack([middle, final]).astype(jnp.bfloat16)
    input_grads = jnp.stack([grad_clips, grad_probe]).astype(jnp.bfloat16)
    grad_first_gain, grad_first_shift, grad_joint_weight, grad_query_bias, grad_value_bias, grad_mixer_weight, grad_mixer_bias, grad_second_gain, grad_second_shift, grad_up_weight, grad_up_bias, grad_down_weight, grad_down_bias = tuple((jnp.stack([one_grad, two_grad]) for one_grad, two_grad in zip(grads_one, grads_two)))
    return (layer_outputs, input_grads, grad_first_gain, grad_first_shift, grad_joint_weight, grad_query_bias, grad_value_bias, grad_mixer_weight, grad_mixer_bias, grad_second_gain, grad_second_shift, grad_up_weight, grad_up_bias, grad_down_weight, grad_down_bias, grad_embed, grad_position)
```

```python
import functools
import jax
import jax.numpy as jnp
from jax import lax
from jax.experimental import pallas as pl
from jax.experimental.pallas import tpu as pltpu
from jax.sharding import PartitionSpec as P
D, HEADS, HD, FF, L = 768, 12, 64, 3072, 512
bf, f32 = jnp.bfloat16, jnp.float32
LOG2E = 1.4426950408889634
SCORE = HD ** (-0.5) * LOG2E
ERF_P = 0.3
ERF_C = (0.11962929578251927, 0.12075400757487373, 0.09991313981909876, 0.12856288726251214,
         -0.05368619840832163, 0.2063564440760747, -0.15720486481493717, 0.035675215624358596)
ANY = pl.BlockSpec(memory_space=pl.ANY)
VM = pl.BlockSpec(memory_space=pltpu.VMEM)
SM = pl.BlockSpec(memory_space=pltpu.SMEM)


def mm(left, right, lc, rc):
    return lax.dot_general(left, right, (((lc,), (rc,)), ((), ())), preferred_element_type=f32)


def gelu_parts(value):
    size = jnp.abs(value)
    t = 1.0 / (1.0 + ERF_P * size)
    total = ERF_C[-1] * t + ERF_C[-2]
    for coefficient in ERF_C[-3::-1]:
        total = total * t + coefficient
    bell = jnp.exp2(value * value * (-0.5 * LOG2E))
    tail = total * t * bell
    phi = jnp.where(value < 0.0, tail, 1.0 - tail)
    return value * phi, phi + value * (bell * 0.3989422804014327)


def norm_stats(rows):
    mean = jnp.mean(rows, axis=1, keepdims=True)
    centered = rows - mean
    rstd = lax.rsqrt(jnp.mean(centered * centered, axis=1, keepdims=True) + 1e-6)
    return centered * rstd, rstd


def norm_back(e, xhat, rstd, gain):
    eg = e * gain
    return (eg - jnp.mean(eg, axis=1, keepdims=True) - xhat * jnp.mean(eg * xhat, axis=1, keepdims=True)) * rstd


class Copies:
    def __init__(self, sems):
        self.sems, self.count, self.pending = sems, 0, []

    def start(self, src, dst):
        copy = pltpu.make_async_copy(src, dst, self.sems.at[self.count])
        self.count += 1
        copy.start()
        return copy

    def out(self, src, dst):
        self.pending.append(self.start(src, dst))

    def finish(self):
        for copy in self.pending:
            copy.wait()


def front(clip, extra, side, x_in, vec, ub, wj_in, wm_in, wu_in, wd_in, *rest):
    outs = rest[extra : extra + 9]
    x, wj, wm, wu, wd, n1, qkv, lt, mixed, after, n2, act, slope, out, sems = rest[extra + 9 :]
    o_n1, o_qkv, o_lt, o_mixed, o_after, o_n2, o_act, o_slope, o_out = outs

    @pl.when(side[0] != 0)
    def _():
        c = Copies(sems)
        cx = c.start(x_in.at[clip] if clip is not None else x_in, x)
        cj = c.start(wj_in, wj)
        cm = c.start(wm_in, wm)
        cu = c.start(wu_in, wu)
        cd = c.start(wd_in, wd)
        g1, s1, qb, vb, mb, g2, s2, db = [vec[i : i + 1, :] for i in range(8)]
        cx.wait()
        xhat, _ = norm_stats(x[...].astype(f32))
        n1[...] = (xhat * g1 + s1).astype(bf)
        c.out(n1, o_n1)
        cj.wait()
        for part, bias in enumerate((qb, None, vb)):
            s = slice(part * D, (part + 1) * D)
            block = mm(n1[...], wj[:, s], 1, 0)
            qkv[:, s] = (block if bias is None else block + bias).astype(bf)
        c.out(qkv, o_qkv)

        lane = lax.broadcasted_iota(jnp.int32, (L, 128), 1)

        def pair(p, logs):
            cols = [pl.ds(pl.multiple_of(p * 128 + part * D, 128), 128) for part in range(3)]
            q, k, v = [qkv[:, s] for s in cols]
            res = []
            for h in range(2):
                qm = jnp.where((lane < 64) == (h == 0), q, jnp.zeros_like(q))
                s = mm(qm, k, 1, 1)
                top = jnp.max(s, axis=1, keepdims=True)
                e = jnp.exp2((s - top) * SCORE)
                total = jnp.sum(e, axis=1, keepdims=True)
                w = (e * (1.0 / total)).astype(bf)
                res.append(mm(w, v, 1, 0))
                logs = jnp.where(lane == 2 * p + h, top * SCORE + jnp.log2(total), logs)
            mixed[:, cols[0]] = jnp.where(lane < 64, res[0], res[1]).astype(bf)
            return logs

        logs = lax.fori_loop(0, HEADS // 2, pair, jnp.zeros((L, 128), f32))
        lt[...] = jnp.transpose(logs)[:16, :]
        c.out(lt, o_lt)
        c.out(mixed, o_mixed)
        cm.wait()
        rows = x[...].astype(f32) + (mm(mixed[...], wm[...], 1, 0) + mb)
        after[...] = rows
        c.out(after, o_after)
        xhat, _ = norm_stats(rows)
        n2[...] = (xhat * g2 + s2).astype(bf)
        c.out(n2, o_n2)
        cu.wait()
        for j in range(FF // D):
            s = slice(j * D, (j + 1) * D)
            for r in range(2):
                rs = slice(r * 256, (r + 1) * 256)
                lifted = mm(n2[rs, :], wu[:, s], 1, 0) + ub[:, s]
                a, b = gelu_parts(lifted)
                act[rs, s] = a.astype(bf)
                slope[rs, s] = b.astype(bf)
        c.out(act, o_act)
        c.out(slope, o_slope)
        cd.wait()
        out[...] = (after[...] + (mm(act[...], wd[...], 1, 0) + db)).astype(bf)
        c.out(out, o_out)
        c.finish()


SAVED = (((L, D), bf), ((L, 3 * D), bf), ((16, L), f32), ((L, D), bf), ((L, D), f32), ((L, D), bf),
         ((L, FF), bf), ((L, FF), bf), ((L, D), bf))


def shapes(spec):
    return [jax.ShapeDtypeStruct(*one) for one in spec]


def scratch(spec):
    return [pltpu.VMEM(*one) for one in spec]


PARAMS = pltpu.CompilerParams(vmem_limit_bytes=62 << 20)


def forward(side, x, clip, vec, ub, weights, old=None):
    extra = 0 if old is None else 9
    xt = ((L, D), x.dtype)
    ws = [(w.shape, w.dtype) for w in weights]
    return pl.pallas_call(
        functools.partial(front, clip, extra),
        out_shape=shapes(SAVED),
        in_specs=[SM, ANY, VM, VM] + [ANY] * (4 + extra),
        out_specs=[ANY] * 9,
        scratch_shapes=scratch([xt] + ws + list(SAVED)) + [pltpu.SemaphoreType.DMA((16,))],
        input_output_aliases={8 + i: i for i in range(extra)},
        compiler_params=PARAMS,
        cost_estimate=pl.CostEstimate(flops=8_050_000_000, bytes_accessed=30_000_000, transcendentals=5_000_000),
    )(side, x, vec, ub, *weights, *(old or ()))


def mlp_back(clip, extra, side, g_in, vec, slope_in, after_in, wu_in, wd_in, *rest):
    o_gl, o_ga, o_vec = rest[extra : extra + 3]
    g, slope, after, wu, wd, gl, ga, vout, sems = rest[extra + 3 :]

    @pl.when(side[0] != 0)
    def _():
        c = Copies(sems)
        cg = c.start(g_in.at[clip] if clip is not None else g_in, g)
        cd = c.start(wd_in, wd)
        cs = c.start(slope_in, slope)
        cu = c.start(wu_in, wu)
        ca = c.start(after_in, after)
        cg.wait()
        cd.wait()
        cs.wait()
        for j in range(FF // D):
            s = slice(j * D, (j + 1) * D)
            piece = (mm(g[...], wd[s, :], 1, 1) * slope[:, s].astype(f32)).astype(bf)
            gl[:, s] = piece
            vout[0:1, s] = jnp.sum(piece.astype(f32), axis=0, keepdims=True)
        c.out(gl, o_gl)
        cu.wait()
        ca.wait()
        e = mm(gl[...], wu[...], 1, 1)
        xhat, rstd = norm_stats(after[...])
        gv = g[...].astype(f32)
        vout[1:2, 0:D] = jnp.sum(e * xhat, axis=0, keepdims=True)
        vout[1:2, D : 2 * D] = jnp.sum(e, axis=0, keepdims=True)
        vout[1:2, 2 * D : 3 * D] = jnp.sum(gv, axis=0, keepdims=True)
        ga[...] = gv + norm_back(e, xhat, rstd, vec[5:6, :])
        c.out(ga, o_ga)
        c.out(vout, o_vec)
        c.finish()


MB_OUT = (((L, FF), bf), ((L, D), f32), ((8, FF), f32))


def backward_mlp(side, g, clip, vec, slope, after, wu, wd, old=None):
    extra = 0 if old is None else 3
    sc = [((L, D), bf), ((L, FF), bf), ((L, D), f32), (wu.shape, bf), (wd.shape, bf)]
    return pl.pallas_call(
        functools.partial(mlp_back, clip, extra),
        out_shape=shapes(MB_OUT),
        in_specs=[SM, ANY, VM] + [ANY] * (4 + extra),
        out_specs=[ANY] * 3,
        scratch_shapes=scratch(sc + list(MB_OUT)) + [pltpu.SemaphoreType.DMA((16,))],
        input_output_aliases={7 + i: i for i in range(extra)},
        compiler_params=PARAMS,
        cost_estimate=pl.CostEstimate(flops=4_830_000_000, bytes_accessed=20_000_000, transcendentals=1000),
    )(side, g, vec, slope, after, wu, wd, *(old or ()))


def attn_back(clip, extra, side, ga_in, x_in, vec, qkv_in, lt_in, wm_in, wj_in, *rest):
    o_gb, o_gj, o_gh, o_vec = rest[extra : extra + 4]
    ga, x, qkv, lt, wm, wj, gm, gb, gj, gh, vout, sems = rest[extra + 4 :]

    @pl.when(side[0] != 0)
    def _():
        c = Copies(sems)
        cg = c.start(ga_in, ga)
        cm = c.start(wm_in, wm)
        cq = c.start(qkv_in, qkv)
        cl = c.start(lt_in, lt)
        cj = c.start(wj_in, wj)
        cx = c.start(x_in.at[clip] if clip is not None else x_in, x)
        cg.wait()
        cm.wait()
        gb[...] = ga[...].astype(bf)
        c.out(gb, o_gb)
        gm[...] = mm(gb[...], wm[...], 1, 1).astype(bf)
        cq.wait()
        cl.wait()
        lane = lax.broadcasted_iota(jnp.int32, (L, 128), 1)

        def pair(p, carry):
            cols = [pl.ds(pl.multiple_of(p * 128 + part * D, 128), 128) for part in range(3)]
            q, k, v = [qkv[:, s] for s in cols]
            go = gm[:, cols[0]]
            res = []
            for h in range(2):
                own = (lane < 64) == (h == 0)
                km = jnp.where(own, k, jnp.zeros_like(k))
                vm = jnp.where(own, v, jnp.zeros_like(v))
                w = jnp.exp2(mm(km, q, 1, 1) * SCORE - lt[pl.ds(2 * p + h, 1), :])
                gw = mm(vm, go, 1, 1)
                inner = jnp.sum(w * gw, axis=0, keepdims=True)
                gs = (w * (gw - inner)).astype(bf)
                res.append((mm(gs, k, 0, 0), mm(gs, q, 1, 0), mm(w.astype(bf), go, 1, 0)))
            for part, scale in enumerate((HD ** (-0.5), HD ** (-0.5), 1.0)):
                both = jnp.where(lane < 64, res[0][part], res[1][part])
                gj[:, cols[part]] = (both * scale).astype(bf)
            return carry

        lax.fori_loop(0, HEADS // 2, pair, 0)
        c.out(gj, o_gj)
        cj.wait()
        cx.wait()
        e = mm(gj[...], wj[...], 1, 1)
        xhat, rstd = norm_stats(x[...].astype(f32))
        vout[0:1, :] = jnp.sum(e * xhat, axis=0, keepdims=True)
        vout[1:2, :] = jnp.sum(e, axis=0, keepdims=True)
        vout[2:3, :] = jnp.sum(gj[:, 0:D].astype(f32), axis=0, keepdims=True)
        vout[3:4, :] = jnp.sum(gj[:, 2 * D :].astype(f32), axis=0, keepdims=True)
        vout[4:5, :] = jnp.sum(gb[...].astype(f32), axis=0, keepdims=True)
        gh[...] = (ga[...] + norm_back(e, xhat, rstd, vec[0:1, :])).astype(gh.dtype)
        c.out(gh, o_gh)
        c.out(vout, o_vec)
        c.finish()


def backward_attn(side, ga, x, clip, vec, qkv, lt, wm, wj, gh_type, old=None):
    extra = 0 if old is None else 3
    outs = (((L, D), bf), ((L, 3 * D), bf), ((L, D), gh_type), ((8, D), f32))
    sc = [((L, D), f32), ((L, D), x.dtype), ((L, 3 * D), bf), ((16, L), f32), (wm.shape, bf), (wj.shape, bf), ((L, D), bf)]
    return pl.pallas_call(
        functools.partial(attn_back, clip, extra),
        out_shape=shapes(outs),
        in_specs=[SM, ANY, ANY, VM] + [ANY] * (4 + extra),
        out_specs=[ANY] * 4,
        scratch_shapes=scratch(sc + list(outs)) + [pltpu.SemaphoreType.DMA((16,))],
        input_output_aliases=dict(zip(range(8, 8 + extra), (0, 1, 3))),
        compiler_params=PARAMS,
        cost_estimate=pl.CostEstimate(flops=4_400_000_000, bytes_accessed=20_000_000, transcendentals=3_000_000),
    )(side, ga, x, vec, qkv, lt, wm, wj, *(old or ()))


def weight_grad(pieces, a0, b0, a1, b1, o_ref, a, b, o, sems):
    c = Copies(sems)
    waits = [c.start(src, dst) for src, dst in ((a0, a.at[0:L]), (a1, a.at[L:]), (b0, b.at[0:L]), (b1, b.at[L:]))]
    for w in waits:
        w.wait()
    rows, cols = o.shape
    if rows > D:
        for j in range(rows // D):
            s = slice(j * D, (j + 1) * D)
            o[s, :] = mm(a[:, s], b[...], 0, 0).astype(bf)
            c.out(o.at[s], o_ref.at[s])
    else:
        for j in range(cols // D):
            s = slice(j * D, (j + 1) * D)
            o[:, s] = mm(a[...], b[:, s], 0, 0).astype(bf)
            c.out(o.at[:, s], o_ref.at[:, s])
    c.finish()


def weight_gradient(a0, b0, a1, b1):
    m, n = a0.shape[1], b0.shape[1]
    return pl.pallas_call(
        functools.partial(weight_grad, None),
        out_shape=jax.ShapeDtypeStruct((m, n), bf),
        in_specs=[ANY] * 4,
        out_specs=ANY,
        scratch_shapes=scratch([((2 * L, m), bf), ((2 * L, n), bf), ((m, n), bf)]) + [pltpu.SemaphoreType.DMA((16,))],
        compiler_params=PARAMS,
        cost_estimate=pl.CostEstimate(flops=4 * L * m * n, bytes_accessed=2 * (2 * L * (m + n) + m * n), transcendentals=0),
    )(a0, b0, a1, b1)


def passed_along(block, distance):
    devices = range(lax.axis_size("section"))
    route = [(i - distance, i) for i in devices if i - distance in devices]
    return lax.ppermute(block, "section", route)


def scatter(values):
    return lax.psum_scatter(values, "batch", scatter_dimension=0, tiled=True)


def shards(clips, mask_flags, mask_embed, pos_embed, first_gain, first_shift, joint_weight, query_bias, value_bias,
           mixer_weight, mixer_bias, second_gain, second_shift, up_weight, up_bias, down_weight, down_bias, out_grad):
    first = lax.axis_index("section") == 0
    lead = first.astype(jnp.int32).reshape(1)
    tail = 1 - lead
    count = lax.axis_size("batch")
    keep = mask_flags.astype(f32)[..., None]
    blended = clips.astype(f32) * (1.0 - keep) + keep * mask_embed + pos_embed
    vec = jnp.concatenate([first_gain, first_shift, query_bias, value_bias, mixer_bias, second_gain, second_shift, down_bias])
    wj, wm, wu, wd = joint_weight[0], mixer_weight[0], up_weight[0], down_weight[0]
    weights = (wj, wm, wu, wd)

    lead0 = forward(lead, blended, 0, vec, up_bias, weights)
    arriving0 = passed_along(lead0[8], 1)
    lead1 = forward(lead, blended, 1, vec, up_bias, weights)
    arriving1 = passed_along(lead1[8], 1)

    def back(side, saved, g, g_clip, x, x_clip, gh_type, old):
        n1, qkv, lt, mixed, after, n2, act, slope, out = saved
        gl, ga, vm = backward_mlp(side, g, g_clip, vec, slope, after, wu, wd, old and old[:3])
        gb, gj, gh, va = backward_attn(side, ga, x, x_clip, vec, qkv, lt, wm, wj, gh_type, old and old[3:])
        return (gl, ga, vm, gb, gj, va), gh

    saved0 = forward(tail, arriving0, None, vec, up_bias, weights, lead0)
    grads0, back0 = back(tail, saved0, out_grad, 0, arriving0, None, bf, None)
    leaving0 = passed_along(back0, -1)
    saved1 = forward(tail, arriving1, None, vec, up_bias, weights, lead1)
    grads1, back1 = back(tail, saved1, out_grad, 1, arriving1, None, bf, None)
    leaving1 = passed_along(back1, -1)
    grads0, blend0 = back(lead, saved0, leaving0, None, blended, 0, f32, grads0)
    g0 = jnp.where(first, leaving0, out_grad[0])
    g1 = jnp.where(first, leaving1, out_grad[1])
    grads1, blend1 = back(lead, saved1, leaving1, None, blended, 1, f32, grads1)

    def pair(i, j):
        return [(a, b) for a, b in ((saved0[i], grads0[j]), (saved1[i], grads1[j]))]

    down = weight_gradient(saved0[6], g0, saved1[6], g1)
    up = weight_gradient(saved0[5], grads0[0], saved1[5], grads1[0])
    joint = weight_gradient(saved0[0], grads0[4], saved1[0], grads1[4])
    mixer = weight_gradient(saved0[3], grads0[3], saved1[3], grads1[3])
    down, up, joint, mixer = [scatter(one).astype(f32)[None] for one in (down, up, joint, mixer)]

    vm = grads0[2] + grads1[2]
    va = grads0[5] + grads1[5]
    columns = [vm[0], vm[1, :D], vm[1, D : 2 * D], vm[1, 2 * D : 3 * D]] + [va[i] for i in range(5)]
    packed = scatter(jnp.concatenate([one.reshape(count, -1) for one in columns], axis=1))
    pieces, at = [], 0
    for one in columns:
        width = one.shape[0] // count
        pieces.append(packed[:, at : at + width])
        at += width
    g_ub, g_gain2, g_shift2, g_db, g_gain1, g_shift1, g_qb, g_vb, g_mb = pieces

    layer_outputs = jnp.stack([saved0[8], saved1[8]])[None]
    blend = jnp.stack([blend0, blend1])
    input_grads = jnp.where(first, blend * (1.0 - keep), jnp.stack([back0, back1]).astype(f32)).astype(bf)[None]
    position = jnp.where(first, blend0 + blend1, 0.0)
    masked = jnp.sum(jnp.where(first, blend * keep, 0.0), axis=(0, 1))
    half = L // 2
    sent_position = passed_along(position[half:].astype(bf), 1).astype(f32)
    sent_masked = passed_along(masked[D // 2 :], 1)
    position = jnp.where(first, position[:half], sent_position)
    masked = jnp.where(first, masked[: D // 2], sent_masked)
    grad_mask, grad_position = lax.psum((masked, position), "batch")
    return (layer_outputs, input_grads, g_gain1, g_shift1, joint, g_qb, g_vb, mixer, g_mb, g_gain2, g_shift2, up, g_ub,
            down, g_db, grad_mask, grad_position)


def solution(mesh):
    whole, section, both = P(), P("section"), P("section", "batch")
    in_specs = (P("batch"), P("batch"), whole, whole) + (section,) * 13 + (P("batch"),)
    out_specs = (both,) * 15 + (section, section)
    return jax.shard_map(shards, mesh=mesh, in_specs=in_specs, out_specs=out_specs, check_vma=False)
```

```python
import functools
import jax
import jax.numpy as jnp
from jax import lax
from jax.experimental import pallas as pl
from jax.experimental.pallas import tpu as pltpu
from jax.sharding import PartitionSpec as P

D, HEADS, HD, FF, L = 768, 12, 64, 3072, 512
bf, f32 = jnp.bfloat16, jnp.float32
LOG2E = 1.4426950408889634
SCORE = HD ** (-0.5) * LOG2E
ERF_P = 0.3
ERF_C = (0.11962929578251927, 0.12075400757487373, 0.09991313981909876, 0.12856288726251214,
         -0.05368619840832163, 0.2063564440760747, -0.15720486481493717, 0.035675215624358596)
ANY = pl.BlockSpec(memory_space=pl.ANY)
VM = pl.BlockSpec(memory_space=pltpu.VMEM)
SM = pl.BlockSpec(memory_space=pltpu.SMEM)


def mm(left, right, lc, rc):
    return lax.dot_general(left, right, (((lc,), (rc,)), ((), ())), preferred_element_type=f32)


def gelu_parts(value):
    size = jnp.abs(value)
    t = 1.0 / (1.0 + ERF_P * size)
    total = ERF_C[-1] * t + ERF_C[-2]
    for coefficient in ERF_C[-3::-1]:
        total = total * t + coefficient
    bell = jnp.exp2(value * value * (-0.5 * LOG2E))
    tail = total * t * bell
    phi = jnp.where(value < 0.0, tail, 1.0 - tail)
    return value * phi, phi + value * (bell * 0.3989422804014327)


def norm_stats(rows):
    mean = jnp.mean(rows, axis=1, keepdims=True)
    centered = rows - mean
    rstd = lax.rsqrt(jnp.mean(centered * centered, axis=1, keepdims=True) + 1e-6)
    return centered * rstd, rstd


def norm_back(e, xhat, rstd, gain):
    eg = e * gain
    return (eg - jnp.mean(eg, axis=1, keepdims=True) - xhat * jnp.mean(eg * xhat, axis=1, keepdims=True)) * rstd


class Copies:
    def __init__(self, sems):
        self.sems, self.count, self.pending = sems, 0, []

    def start(self, src, dst):
        copy = pltpu.make_async_copy(src, dst, self.sems.at[self.count])
        self.count += 1
        copy.start()
        return copy

    def out(self, src, dst):
        self.pending.append(self.start(src, dst))

    def finish(self):
        for copy in self.pending:
            copy.wait()


def front(clip, extra, side, x_in, vec, ub, wj_in, wm_in, wu_in, wd_in, *rest):
    outs = rest[extra : extra + 9]
    x, wj, wm, wu, wd, n1, qkv, lt, mixed, after, n2, act, slope, out, sems = rest[extra + 9 :]
    o_n1, o_qkv, o_lt, o_mixed, o_after, o_n2, o_act, o_slope, o_out = outs

    @pl.when(side[0] != 0)
    def _():
        c = Copies(sems)
        cx = c.start(x_in.at[clip] if clip is not None else x_in, x)
        cj = c.start(wj_in, wj)
        cm = c.start(wm_in, wm)
        cu = c.start(wu_in, wu)
        cd = c.start(wd_in, wd)
        g1, s1, qb, vb, mb, g2, s2, db = [vec[i : i + 1, :] for i in range(8)]
        cx.wait()
        xhat, _ = norm_stats(x[...].astype(f32))
        n1[...] = (xhat * g1 + s1).astype(bf)
        c.out(n1, o_n1)
        cj.wait()
        for part, bias in enumerate((qb, None, vb)):
            s = slice(part * D, (part + 1) * D)
            block = mm(n1[...], wj[:, s], 1, 0)
            qkv[:, s] = (block if bias is None else block + bias).astype(bf)
        c.out(qkv, o_qkv)

        lane = lax.broadcasted_iota(jnp.int32, (L, 128), 1)

        def pair(p, logs):
            cols = [pl.ds(pl.multiple_of(p * 128 + part * D, 128), 128) for part in range(3)]
            q, k, v = [qkv[:, s] for s in cols]
            res = []
            for h in range(2):
                qm = jnp.where((lane < 64) == (h == 0), q, jnp.zeros_like(q))
                s = mm(qm, k, 1, 1)
                top = jnp.max(s, axis=1, keepdims=True)
                e = jnp.exp2((s - top) * SCORE)
                total = jnp.sum(e, axis=1, keepdims=True)
                w = (e * (1.0 / total)).astype(bf)
                res.append(mm(w, v, 1, 0))
                logs = jnp.where(lane == 2 * p + h, top * SCORE + jnp.log2(total), logs)
            mixed[:, cols[0]] = jnp.where(lane < 64, res[0], res[1]).astype(bf)
            return logs

        logs = lax.fori_loop(0, HEADS // 2, pair, jnp.zeros((L, 128), f32))
        lt[...] = jnp.transpose(logs)[:16, :]
        c.out(lt, o_lt)
        c.out(mixed, o_mixed)
        cm.wait()
        rows = x[...].astype(f32) + (mm(mixed[...], wm[...], 1, 0) + mb)
        after[...] = rows
        c.out(after, o_after)
        xhat, _ = norm_stats(rows)
        n2[...] = (xhat * g2 + s2).astype(bf)
        c.out(n2, o_n2)
        cu.wait()
        for j in range(FF // D):
            s = slice(j * D, (j + 1) * D)
            for r in range(2):
                rs = slice(r * 256, (r + 1) * 256)
                lifted = mm(n2[rs, :], wu[:, s], 1, 0) + ub[:, s]
                a, b = gelu_parts(lifted)
                act[rs, s] = a.astype(bf)
                slope[rs, s] = b.astype(bf)
        c.out(act, o_act)
        c.out(slope, o_slope)
        cd.wait()
        out[...] = (after[...] + (mm(act[...], wd[...], 1, 0) + db)).astype(bf)
        c.out(out, o_out)
        c.finish()


SAVED = (((L, D), bf), ((L, 3 * D), bf), ((16, L), f32), ((L, D), bf), ((L, D), f32), ((L, D), bf),
         ((L, FF), bf), ((L, FF), bf), ((L, D), bf))


def shapes(spec):
    return [jax.ShapeDtypeStruct(*one) for one in spec]


def scratch(spec):
    return [pltpu.VMEM(*one) for one in spec]


PARAMS = pltpu.CompilerParams(vmem_limit_bytes=62 << 20)


def forward(side, x, clip, vec, ub, weights, old=None):
    extra = 0 if old is None else 9
    xt = ((L, D), x.dtype)
    ws = [(w.shape, w.dtype) for w in weights]
    return pl.pallas_call(
        functools.partial(front, clip, extra),
        out_shape=shapes(SAVED),
        in_specs=[SM, ANY, VM, VM] + [ANY] * (4 + extra),
        out_specs=[ANY] * 9,
        scratch_shapes=scratch([xt] + ws + list(SAVED)) + [pltpu.SemaphoreType.DMA((16,))],
        input_output_aliases={8 + i: i for i in range(extra)},
        compiler_params=PARAMS,
        cost_estimate=pl.CostEstimate(flops=8_050_000_000, bytes_accessed=30_000_000, transcendentals=5_000_000),
    )(side, x, vec, ub, *weights, *(old or ()))


def mlp_back(clip, extra, side, g_in, vec, slope_in, after_in, wu_in, wd_in, *rest):
    o_gl, o_ga, o_vec = rest[extra : extra + 3]
    g, slope, after, wu, wd, gl, ga, vout, sems = rest[extra + 3 :]

    @pl.when(side[0] != 0)
    def _():
        c = Copies(sems)
        cg = c.start(g_in.at[clip] if clip is not None else g_in, g)
        cd = c.start(wd_in, wd)
        cs = c.start(slope_in, slope)
        cu = c.start(wu_in, wu)
        ca = c.start(after_in, after)
        cg.wait()
        cd.wait()
        cs.wait()
        for j in range(FF // D):
            s = slice(j * D, (j + 1) * D)
            piece = (mm(g[...], wd[s, :], 1, 1) * slope[:, s].astype(f32)).astype(bf)
            gl[:, s] = piece
            vout[0:1, s] = jnp.sum(piece.astype(f32), axis=0, keepdims=True)
        c.out(gl, o_gl)
        cu.wait()
        ca.wait()
        e = mm(gl[...], wu[...], 1, 1)
        xhat, rstd = norm_stats(after[...])
        gv = g[...].astype(f32)
        vout[1:2, 0:D] = jnp.sum(e * xhat, axis=0, keepdims=True)
        vout[1:2, D : 2 * D] = jnp.sum(e, axis=0, keepdims=True)
        vout[1:2, 2 * D : 3 * D] = jnp.sum(gv, axis=0, keepdims=True)
        ga[...] = gv + norm_back(e, xhat, rstd, vec[5:6, :])
        c.out(ga, o_ga)
        c.out(vout, o_vec)
        c.finish()


MB_OUT = (((L, FF), bf), ((L, D), f32), ((8, FF), f32))


def backward_mlp(side, g, clip, vec, slope, after, wu, wd, old=None):
    extra = 0 if old is None else 3
    sc = [((L, D), bf), ((L, FF), bf), ((L, D), f32), (wu.shape, bf), (wd.shape, bf)]
    return pl.pallas_call(
        functools.partial(mlp_back, clip, extra),
        out_shape=shapes(MB_OUT),
        in_specs=[SM, ANY, VM] + [ANY] * (4 + extra),
        out_specs=[ANY] * 3,
        scratch_shapes=scratch(sc + list(MB_OUT)) + [pltpu.SemaphoreType.DMA((16,))],
        input_output_aliases={7 + i: i for i in range(extra)},
        compiler_params=PARAMS,
        cost_estimate=pl.CostEstimate(flops=4_830_000_000, bytes_accessed=20_000_000, transcendentals=1000),
    )(side, g, vec, slope, after, wu, wd, *(old or ()))


def attn_back(clip, lead, extra, side, ga_in, x_in, vec, flags, qkv_in, lt_in, wm_in, wj_in, *rest):
    o_gb, o_gj, o_gh, o_vec = rest[extra : extra + 4]
    rest = rest[extra + 4 :]
    if lead:
        o_full, full, rest = rest[0], rest[-2], rest[1:-2] + rest[-1:]
    ga, x, qkv, lt, wm, wj, gm, gb, gj, gh, vout, sems = rest

    @pl.when(side[0] != 0)
    def _():
        c = Copies(sems)
        cg = c.start(ga_in, ga)
        cm = c.start(wm_in, wm)
        cq = c.start(qkv_in, qkv)
        cl = c.start(lt_in, lt)
        cj = c.start(wj_in, wj)
        cx = c.start(x_in.at[clip] if clip is not None else x_in, x)
        cg.wait()
        cm.wait()
        gb[...] = ga[...].astype(bf)
        c.out(gb, o_gb)
        gm[...] = mm(gb[...], wm[...], 1, 1).astype(bf)
        cq.wait()
        cl.wait()
        lane = lax.broadcasted_iota(jnp.int32, (L, 128), 1)

        def pair(p, carry):
            cols = [pl.ds(pl.multiple_of(p * 128 + part * D, 128), 128) for part in range(3)]
            q, k, v = [qkv[:, s] for s in cols]
            go = gm[:, cols[0]]
            res = []
            for h in range(2):
                own = (lane < 64) == (h == 0)
                km = jnp.where(own, k, jnp.zeros_like(k))
                vm = jnp.where(own, v, jnp.zeros_like(v))
                w = jnp.exp2(mm(km, q, 1, 1) * SCORE - lt[pl.ds(2 * p + h, 1), :])
                gw = mm(vm, go, 1, 1)
                inner = jnp.sum(w * gw, axis=0, keepdims=True)
                gs = (w * (gw - inner)).astype(bf)
                res.append((mm(gs, k, 0, 0), mm(gs, q, 1, 0), mm(w.astype(bf), go, 1, 0)))
            for part, scale in enumerate((HD ** (-0.5), HD ** (-0.5), 1.0)):
                both = jnp.where(lane < 64, res[0][part], res[1][part])
                gj[:, cols[part]] = (both * scale).astype(bf)
            return carry

        lax.fori_loop(0, HEADS // 2, pair, 0)
        c.out(gj, o_gj)
        cj.wait()
        cx.wait()
        e = mm(gj[...], wj[...], 1, 1)
        xhat, rstd = norm_stats(x[...].astype(f32))
        vout[0:1, :] = jnp.sum(e * xhat, axis=0, keepdims=True)
        vout[1:2, :] = jnp.sum(e, axis=0, keepdims=True)
        vout[2:3, :] = jnp.sum(gj[:, 0:D].astype(f32), axis=0, keepdims=True)
        vout[3:4, :] = jnp.sum(gj[:, 2 * D :].astype(f32), axis=0, keepdims=True)
        vout[4:5, :] = jnp.sum(gb[...].astype(f32), axis=0, keepdims=True)
        whole = ga[...] + norm_back(e, xhat, rstd, vec[0:1, :])
        if lead:
            free = whole * (1.0 - flags[clip].astype(f32))
            full[...] = whole
            c.out(full, o_full)
            vout[5:6, :] = jnp.sum(whole - free, axis=0, keepdims=True)
            whole = free
        gh[...] = whole.astype(bf)
        c.out(gh, o_gh)
        c.out(vout, o_vec)
        c.finish()


def backward_attn(side, ga, x, clip, vec, flags, qkv, lt, wm, wj, old=None):
    lead = old is not None
    extra = 4 if lead else 0
    outs = (((L, D), bf), ((L, 3 * D), bf), ((L, D), bf), ((8, D), f32))
    full = (((L, D), f32),) if lead else ()
    sc = [((L, D), f32), ((L, D), x.dtype), ((L, 3 * D), bf), ((16, L), f32), (wm.shape, bf), (wj.shape, bf), ((L, D), bf)]
    return pl.pallas_call(
        functools.partial(attn_back, clip, lead, extra),
        out_shape=shapes(outs + full),
        in_specs=[SM, ANY, ANY, VM, VM] + [ANY] * (4 + extra),
        out_specs=[ANY] * (4 + lead),
        scratch_shapes=scratch(sc + list(outs + full)) + [pltpu.SemaphoreType.DMA((16,))],
        input_output_aliases={9 + i: i for i in range(extra)},
        compiler_params=PARAMS,
        cost_estimate=pl.CostEstimate(flops=4_400_000_000, bytes_accessed=20_000_000, transcendentals=3_000_000),
    )(side, ga, x, vec, flags, qkv, lt, wm, wj, *(old or ()))


def weight_grad(a0, b0, a1, b1, o_ref, a, b, o, sems):
    c = Copies(sems)
    waits = [c.start(src, dst) for src, dst in ((a0, a.at[0:L]), (a1, a.at[L:]), (b0, b.at[0:L]), (b1, b.at[L:]))]
    for w in waits:
        w.wait()
    rows, cols = o.shape
    if rows > D:
        for j in range(rows // D):
            s = slice(j * D, (j + 1) * D)
            o[s, :] = mm(a[:, s], b[...], 0, 0).astype(bf)
            c.out(o.at[s], o_ref.at[s])
    else:
        for j in range(cols // D):
            s = slice(j * D, (j + 1) * D)
            o[:, s] = mm(a[...], b[:, s], 0, 0).astype(bf)
            c.out(o.at[:, s], o_ref.at[:, s])
    c.finish()


def weight_gradient(a0, b0, a1, b1):
    m, n = a0.shape[1], b0.shape[1]
    return pl.pallas_call(
        weight_grad,
        out_shape=jax.ShapeDtypeStruct((m, n), bf),
        in_specs=[ANY] * 4,
        out_specs=ANY,
        scratch_shapes=scratch([((2 * L, m), bf), ((2 * L, n), bf), ((m, n), bf)]) + [pltpu.SemaphoreType.DMA((16,))],
        compiler_params=PARAMS,
        cost_estimate=pl.CostEstimate(flops=4 * L * m * n, bytes_accessed=2 * (2 * L * (m + n) + m * n), transcendentals=0),
    )(a0, b0, a1, b1)


def passed_along(block, distance):
    devices = range(lax.axis_size("section"))
    route = [(i - distance, i) for i in devices if i - distance in devices]
    return lax.ppermute(block, "section", route)


def scatter(values):
    return lax.psum_scatter(values, "batch", scatter_dimension=0, tiled=True)


def split_grad(kind, count, part, *refs):
    ins, (keep, send), (a, b, o, sems) = refs[:-6], refs[-6:-4], refs[-4:]
    c = Copies(sems)
    mine = part[0]

    def load(pairs):
        return [c.start(src, dst) for src, dst in pairs]

    if kind == "down":
        a0, b0, a1, b1, other = ins
        waits = load(((a0, a.at[0:L]), (a1, a.at[L:])))
        rows = (b.at[0:L], b.at[L:])

        @pl.when(part[1] != 0)
        def _():
            for src, dst, sem in zip((b0, b1), rows, (18, 19)):
                pltpu.make_async_copy(src, dst, sems.at[sem]).start()

        @pl.when(part[1] == 0)
        def _():
            for at, dst, sem in zip((0, 1), rows, (18, 19)):
                pltpu.make_async_copy(other.at[at], dst, sems.at[sem]).start()

        for src, dst, sem in zip((b0, b1), rows, (18, 19)):
            pltpu.make_async_copy(src, dst, sems.at[sem]).wait()
        for w in waits:
            w.wait()
        height = FF // count
        per = D // height // 2
        for j in range(FF // D):
            tile = mm(a[:, j * D : (j + 1) * D], b[...], 0, 0).astype(bf)
            for i in range(2 * per):
                o[i % 2, j * per + i // 2] = tile[i * height : (i + 1) * height]
            s = slice(j * per, (j + 1) * per)
            c.out(o.at[mine, s], keep.at[s])
            c.out(o.at[1 - mine, s], send.at[s])
    else:
        height = D // count
        groups = [ins[i : i + 4] for i in range(0, len(ins), 4)]
        loads = []
        column = 0
        for g, (a0, b0, a1, b1) in enumerate(groups):
            width = b0.shape[1]
            r = slice(column, column + width)
            l = slice(g * D, (g + 1) * D)
            loads.append(load(((a0, a.at[0:L, l]), (a1, a.at[L:, l]), (b0, b.at[0:L, r]), (b1, b.at[L:, r]))))
            column += width
        t = 0
        for g, (a0, b0, a1, b1) in enumerate(groups):
            for w in loads[g]:
                w.wait()
            for _ in range(b0.shape[1] // D):
                tile = mm(a[:, g * D : (g + 1) * D], b[:, t * D : (t + 1) * D], 0, 0).astype(bf)
                for i in range(count):
                    o[i % 2, i // 2, t * height : (t + 1) * height] = tile[i * height : (i + 1) * height]
                t += 1
        c.out(o.at[mine], keep)
        c.out(o.at[1 - mine], send)
    c.finish()


def split_gradient(kind, count, part, groups):
    flat = [one for group in groups for one in group]
    pairs = groups if kind == "both" else groups[:1]
    m = sum(group[0].shape[1] for group in pairs)
    n = sum(group[1].shape[1] for group in pairs)
    half = jax.ShapeDtypeStruct((count // 2, 4 * D // count, D), bf)
    return pl.pallas_call(
        functools.partial(split_grad, kind, count),
        out_shape=(half, half),
        in_specs=[SM] + [ANY] * len(flat),
        out_specs=(ANY, ANY),
        scratch_shapes=scratch([((2 * L, m), bf), ((2 * L, n), bf), ((2,) + half.shape, bf)]) + [pltpu.SemaphoreType.DMA((20,))],
        compiler_params=PARAMS,
        cost_estimate=pl.CostEstimate(flops=16 * L * D * D, bytes_accessed=2 * (2 * L * (m + n) + 4 * D * D), transcendentals=0),
    )(part, *flat)


def swapped(values, bit):
    return lax.ppermute(values, "batch", [(i, i ^ bit) for i in range(lax.axis_size("batch"))])


def added(left, right):
    return left.astype(f32) + right.astype(f32)


def after(value, *others):
    return lax.optimization_barrier((value,) + others)


def halve(keep, send, place, level):
    came = swapped(send, 1 << level)
    if keep.shape[0] == 1:
        return added(keep[0], came[0])
    own = (place >> (level + 1)) & 1
    shape = (keep.shape[0] // 2, 2) + keep.shape[1:]
    kept, got = keep.reshape(shape), came.reshape(shape)

    def pick(side):
        return added(lax.dynamic_index_in_dim(kept, side, 1, False), lax.dynamic_index_in_dim(got, side, 1, False)).astype(bf)

    return pick(own), pick(1 - own)


def summed(values, place):
    levels = lax.axis_size("batch").bit_length() - 1
    cut = [level for level in (2, 3) if level < levels]

    def exchange(block, level):
        return swapped(block, 1 << level)

    values = added(values, exchange(values, 0)).astype(bf)
    for level in cut:
        own = (place >> level) & 1
        parts = values.reshape(2, -1, D)
        came = exchange(lax.dynamic_index_in_dim(parts, 1 - own, 0, False), level)
        values = added(lax.dynamic_index_in_dim(parts, own, 0, False), came).astype(bf)
    for level in range(1, levels):
        if level not in cut:
            values = added(values, exchange(values, level)).astype(bf)
    for level in reversed(cut):
        own = (place >> level) & 1
        came = exchange(values, level)
        low, high = jnp.where(own == 0, values, came), jnp.where(own == 0, came, values)
        values = jnp.concatenate([low, high])
    return values


def collect_small(flag, b0, b1, v0, v1, a0, a1, here, moved):
    half = L // 2
    for out, s in ((here, slice(0, half)), (moved, slice(half, L))):
        out[0:half, :] = (b0[s, :] + b1[s, :]).astype(bf)
        out[half:, :] = jnp.zeros((64, D), bf)
    vm = v0[...] + v1[...]
    va = a0[...] + a1[...]
    for out in (here, moved):
        out[half : half + 1, :] = va[5:6].astype(bf)
    block = jnp.concatenate([vm[0:1, i * D : (i + 1) * D] for i in range(4)] + [vm[1:2, i * D : (i + 1) * D] for i in range(3)]
                            + [va[i : i + 1] for i in range(5)] + [jnp.zeros((4, D), f32)])
    here[half + 16 : half + 32, :] = block.astype(bf)


def collect(*values):
    half = jax.ShapeDtypeStruct((L // 2 + 64, D), bf)
    return pl.pallas_call(
        collect_small,
        out_shape=(half, half),
        in_specs=[SM] + [VM] * 6,
        out_specs=(VM, VM),
        cost_estimate=pl.CostEstimate(flops=1_000_000, bytes_accessed=5_000_000, transcendentals=0),
    )(*values)


def passed_along(block, distance):
    devices = range(lax.axis_size("section"))
    route = [(i - distance, i) for i in devices if i - distance in devices]
    return lax.ppermute(block, "section", route)


def scatter(values):
    return lax.psum_scatter(values, "batch", scatter_dimension=0, tiled=True)


def split_grad(kind, count, part, *refs):
    ins, (keep, send), (a, b, o, sems) = refs[:-6], refs[-6:-4], refs[-4:]
    c = Copies(sems)
    mine = part[0]

    def load(pairs):
        return [c.start(src, dst) for src, dst in pairs]

    if kind == "down":
        a0, b0, a1, b1, other = ins
        waits = load(((a0, a.at[0:L]), (a1, a.at[L:])))
        rows = (b.at[0:L], b.at[L:])

        @pl.when(part[1] != 0)
        def _():
            for src, dst, sem in zip((b0, b1), rows, (18, 19)):
                pltpu.make_async_copy(src, dst, sems.at[sem]).start()

        @pl.when(part[1] == 0)
        def _():
            for at, dst, sem in zip((0, 1), rows, (18, 19)):
                pltpu.make_async_copy(other.at[at], dst, sems.at[sem]).start()

        for src, dst, sem in zip((b0, b1), rows, (18, 19)):
            pltpu.make_async_copy(src, dst, sems.at[sem]).wait()
        for w in waits:
            w.wait()
        height = FF // count
        per = D // height // 2
        for j in range(FF // D):
            tile = mm(a[:, j * D : (j + 1) * D], b[...], 0, 0).astype(bf)
            for i in range(2 * per):
                o[i % 2, j * per + i // 2] = tile[i * height : (i + 1) * height]
            s = slice(j * per, (j + 1) * per)
            c.out(o.at[mine, s], keep.at[s])
            c.out(o.at[1 - mine, s], send.at[s])
    else:
        height = D // count
        groups = [ins[i : i + 4] for i in range(0, len(ins), 4)]
        loads = []
        column = 0
        for g, (a0, b0, a1, b1) in enumerate(groups):
            width = b0.shape[1]
            r = slice(column, column + width)
            l = slice(g * D, (g + 1) * D)
            loads.append(load(((a0, a.at[0:L, l]), (a1, a.at[L:, l]), (b0, b.at[0:L, r]), (b1, b.at[L:, r]))))
            column += width
        t = 0
        for g, (a0, b0, a1, b1) in enumerate(groups):
            for w in loads[g]:
                w.wait()
            for _ in range(b0.shape[1] // D):
                tile = mm(a[:, g * D : (g + 1) * D], b[:, t * D : (t + 1) * D], 0, 0).astype(bf)
                for i in range(count):
                    o[i % 2, i // 2, t * height : (t + 1) * height] = tile[i * height : (i + 1) * height]
                t += 1
        c.out(o.at[mine], keep)
        c.out(o.at[1 - mine], send)
    c.finish()


def split_gradient(kind, count, part, groups):
    flat = [one for group in groups for one in group]
    pairs = groups if kind == "both" else groups[:1]
    m = sum(group[0].shape[1] for group in pairs)
    n = sum(group[1].shape[1] for group in pairs)
    half = jax.ShapeDtypeStruct((count // 2, 4 * D // count, D), bf)
    return pl.pallas_call(
        functools.partial(split_grad, kind, count),
        out_shape=(half, half),
        in_specs=[SM] + [ANY] * len(flat),
        out_specs=(ANY, ANY),
        scratch_shapes=scratch([((2 * L, m), bf), ((2 * L, n), bf), ((2,) + half.shape, bf)]) + [pltpu.SemaphoreType.DMA((20,))],
        compiler_params=PARAMS,
        cost_estimate=pl.CostEstimate(flops=16 * L * D * D, bytes_accessed=2 * (2 * L * (m + n) + 4 * D * D), transcendentals=0),
    )(part, *flat)


def swapped(values, bit):
    return lax.ppermute(values, "batch", [(i, i ^ bit) for i in range(lax.axis_size("batch"))])


def added(left, right):
    return left.astype(f32) + right.astype(f32)


def shards(clips, mask_flags, mask_embed, pos_embed, first_gain, first_shift, joint_weight, query_bias, value_bias,
           mixer_weight, mixer_bias, second_gain, second_shift, up_weight, up_bias, down_weight, down_bias, out_grad):
    first = lax.axis_index("section") == 0
    lead = first.astype(jnp.int32).reshape(1)
    tail = 1 - lead
    count = lax.axis_size("batch")
    keep = mask_flags.astype(f32)[..., None]
    blended = clips.astype(f32) * (1.0 - keep) + keep * mask_embed + pos_embed
    vec = jnp.concatenate([first_gain, first_shift, query_bias, value_bias, mixer_bias, second_gain, second_shift, down_bias])
    wj, wm, wu, wd = joint_weight[0], mixer_weight[0], up_weight[0], down_weight[0]
    weights = (wj, wm, wu, wd)

    flags = mask_flags[..., None]
    place = lax.axis_index("batch")
    part = jnp.stack([place % 2, lead[0]]).astype(jnp.int32)
    fast = (D // count) % 16 == 0

    def handed(block, distance):
        return passed_along(block, distance)

    lead0 = forward(lead, blended, 0, vec, up_bias, weights)
    arriving0 = handed(lead0[8], 1)
    lead1 = forward(lead, blended, 1, vec, up_bias, weights)
    arriving1 = handed(lead1[8], 1)

    def back(side, saved, g, x, clip, old):
        _, qkv, lt, _, after_rows, _, _, slope, _ = saved
        own = clip if old is None else None
        gl, ga, vm = backward_mlp(side, g, own, vec, slope, after_rows, wu, wd, old and old[:3])
        at = None if old is None else clip
        gb, gj, gh, va, *full = backward_attn(side, ga, x, at, vec, flags, qkv, lt, wm, wj, old and old[3:])
        return (gl, ga, vm, gb, gj, gh, va), full

    saved0 = forward(tail, arriving0, None, vec, up_bias, weights, lead0)
    grads0, _ = back(tail, saved0, out_grad, arriving0, 0, None)
    leaving0 = handed(grads0[5], -1)
    saved1 = forward(tail, arriving1, None, vec, up_bias, weights, lead1)
    grads1, _ = back(tail, saved1, out_grad, arriving1, 1, None)
    leaving1 = handed(grads1[5], -1)
    grads0, (blend0,) = back(lead, saved0, leaving0, blended, 0, grads0)
    va0 = grads0[6]

    n1_1, qkv_1, lt_1, mixed_1, after_1, n2_1, act_1, slope_1, _ = saved1
    if fast:
        part_d, va0 = after(part, va0)
        down = split_gradient("down", count, part_d, [(saved0[6], leaving0, act_1, leaving1, out_grad)])
        lead_m, *down = after(lead, *down)
        gl1, ga1, vm1 = backward_mlp(lead_m, leaving1, None, vec, slope_1, after_1, wu, wd, grads1[:3])
        down = halve(*down, place, 0)
        part_u, *down = after(part, *down)
        up = split_gradient("up", count, part_u, [(saved0[5], grads0[0], n2_1, gl1)])
        lead_a, *up = after(lead, *up)
    else:
        gl1, ga1, vm1 = backward_mlp(lead, leaving1, None, vec, slope_1, after_1, wu, wd, grads1[:3])
        lead_a = lead
    gb1, gj1, gh1, va1, blend1 = backward_attn(lead_a, ga1, blended, 1, vec, flags, qkv_1, lt_1, wm, wj, grads1[3:])
    here, moved = collect(lead, blend0, blend1, grads0[2], vm1, va0, va1)
    joint_group, mixer_group = (saved0[0], grads0[4], n1_1, gj1), (saved0[3], grads0[3], mixed_1, gb1)
    if fast:
        up = halve(*up, place, 0)
        down = halve(*down, place, 1)
        part_b, *rest = after(part, *up, *down)
        up, down = rest[:2], rest[2:]
        both = split_gradient("both", count, part_b, [joint_group, mixer_group])
        levels = count.bit_length() - 1
        down, up, both = [functools.reduce(lambda pair, level: halve(*pair, place, level), range(at, levels), value)
                          for at, value in ((2, down), (1, up), (0, both))]
        height = D // count

        def wide(block):
            return jnp.swapaxes(block.reshape(-1, height, D), 0, 1).reshape(height, -1)

        up, joint, mixer = wide(up), wide(both[: 3 * height]), both[3 * height :]
    else:
        g0 = jnp.where(first, leaving0, out_grad[0])
        g1 = jnp.where(first, leaving1, out_grad[1])
        down_group, up_group = (saved0[6], g0, act_1, g1), (saved0[5], grads0[0], n2_1, gl1)
        down, up, joint, mixer = [
            scatter(weight_gradient(*group)).astype(f32) for group in (down_group, up_group, joint_group, mixer_group)
        ]
    down, up, joint, mixer = [one[None] for one in (down, up, joint, mixer)]

    layer_outputs = jnp.stack([saved0[8], saved1[8]])[None]
    input_grads = jnp.stack([grads0[5], gh1])[None]
    half = L // 2
    arrived = handed(moved, 1)[: half + 16]
    top = jnp.where(first, here[: half + 16], arrived)
    total = summed(jnp.concatenate([top, here[half + 16 :]]), place).astype(f32)
    grad_position = total[:half]
    grad_mask = lax.dynamic_slice(total[half], (jnp.where(first, 0, D // 2),), (D // 2,))
    sums = total[half + 16 :]
    g_ub = lax.dynamic_slice(sums[:4].reshape(1, FF), (0, place * (FF // count)), (1, FF // count))
    rest = lax.dynamic_slice(sums[4:12], (0, place * (D // count)), (8, D // count))
    g_gain2, g_shift2, g_db, g_gain1, g_shift1, g_qb, g_vb, g_mb = [rest[i : i + 1] for i in range(8)]
    return (layer_outputs, input_grads, g_gain1, g_shift1, joint, g_qb, g_vb, mixer, g_mb, g_gain2, g_shift2, up, g_ub,
            down, g_db, grad_mask, grad_position)


def solution(mesh):
    whole, section, both = P(), P("section"), P("section", "batch")
    in_specs = (P("batch"), P("batch"), whole, whole) + (section,) * 13 + (P("batch"),)
    out_specs = (both,) * 15 + (section, section)

    def step(*arrays):
        return shards(*arrays)

    step = jax.shard_map(step, mesh=mesh, in_specs=in_specs, out_specs=out_specs, check_vma=False)
    return step
```

```python
import functools
import jax
import jax.numpy as jnp
from jax import lax
from jax.experimental import pallas as pl
from jax.experimental.pallas import tpu as pltpu
from jax.sharding import PartitionSpec as P

D, HEADS, HD, FF, L = 768, 12, 64, 3072, 512
bf, f32 = jnp.bfloat16, jnp.float32
LOG2E = 1.4426950408889634
SCORE = HD ** (-0.5) * LOG2E
ERF_P = 0.3
ERF_C = (0.11962929578251927, 0.12075400757487373, 0.09991313981909876, 0.12856288726251214,
         -0.05368619840832163, 0.2063564440760747, -0.15720486481493717, 0.035675215624358596)
ANY = pl.BlockSpec(memory_space=pl.ANY)
VM = pl.BlockSpec(memory_space=pltpu.VMEM)
SM = pl.BlockSpec(memory_space=pltpu.SMEM)


def mm(left, right, lc, rc):
    return lax.dot_general(left, right, (((lc,), (rc,)), ((), ())), preferred_element_type=f32)


def gelu_parts(value):
    size = jnp.abs(value)
    t = pl.reciprocal(1.0 + ERF_P * size)
    total = ERF_C[-1] * t + ERF_C[-2]
    for coefficient in ERF_C[-3::-1]:
        total = total * t + coefficient
    bell = jnp.exp2(value * value * (-0.5 * LOG2E))
    tail = total * t * bell
    phi = jnp.where(value < 0.0, tail, 1.0 - tail)
    return value * phi, phi + value * (bell * 0.3989422804014327)


def norm_stats(rows):
    mean = jnp.mean(rows, axis=1, keepdims=True)
    centered = rows - mean
    rstd = lax.rsqrt(jnp.mean(centered * centered, axis=1, keepdims=True) + 1e-6)
    return centered * rstd, rstd


def norm_back(e, xhat, rstd, gain):
    eg = e * gain
    return (eg - jnp.mean(eg, axis=1, keepdims=True) - xhat * jnp.mean(eg * xhat, axis=1, keepdims=True)) * rstd


class Copies:
    def __init__(self, sems):
        self.sems, self.count, self.pending = sems, 0, []

    def start(self, src, dst):
        copy = pltpu.make_async_copy(src, dst, self.sems.at[self.count])
        self.count += 1
        copy.start()
        return copy

    def out(self, src, dst):
        self.pending.append(self.start(src, dst))

    def finish(self):
        for copy in self.pending:
            copy.wait()


def front(clip, extra, side, x_in, vec, ub, wj_in, wm_in, wu_in, wd_in, *rest):
    outs = rest[extra : extra + 9]
    x, wj, wm, wu, wd, n1, qkv, lt, mixed, after, n2, act, slope, out, sems = rest[extra + 9 :]
    o_n1, o_qkv, o_lt, o_mixed, o_after, o_n2, o_act, o_slope, o_out = outs

    @pl.when(side[0] != 0)
    def _():
        c = Copies(sems)
        cx = c.start(x_in.at[clip] if clip is not None else x_in, x)
        parts = [slice(i * D, (i + 1) * D) for i in range(3)]
        cj = [c.start(wj_in.at[:, s], wj.at[:, s]) for s in parts]
        g1, s1, qb, vb, mb, g2, s2, db = [vec[i : i + 1, :] for i in range(8)]
        cx.wait()
        xhat, _ = norm_stats(x[...].astype(f32))
        n1[...] = (xhat * g1 + s1).astype(bf)
        c.out(n1, o_n1)
        for s, copy, bias in zip(parts, cj, (qb, None, vb)):
            copy.wait()
            block = mm(n1[...], wj[:, s], 1, 0)
            qkv[:, s] = (block if bias is None else block + bias).astype(bf)
        c.out(qkv, o_qkv)
        cm = c.start(wm_in, wm)
        cu = c.start(wu_in, wu)
        cd = c.start(wd_in, wd)

        lane = lax.broadcasted_iota(jnp.int32, (L, 128), 1)

        def pair(p, logs):
            cols = [pl.ds(pl.multiple_of(p * 128 + part * D, 128), 128) for part in range(3)]
            q, k, v = [qkv[:, s] for s in cols]
            res = []
            for h in range(2):
                qm = jnp.where((lane < 64) == (h == 0), q, jnp.zeros_like(q))
                s = mm(qm, k, 1, 1)
                top = jnp.max(s, axis=1, keepdims=True)
                e = jnp.exp2((s - top) * SCORE)
                total = jnp.sum(e, axis=1, keepdims=True)
                w = (e * (1.0 / total)).astype(bf)
                res.append(mm(w, v, 1, 0))
                logs = jnp.where(lane == 2 * p + h, top * SCORE + jnp.log2(total), logs)
            mixed[:, cols[0]] = jnp.where(lane < 64, res[0], res[1]).astype(bf)
            return logs

        logs = lax.fori_loop(0, HEADS // 2, pair, jnp.zeros((L, 128), f32))
        lt[...] = jnp.transpose(logs)[:16, :]
        c.out(lt, o_lt)
        c.out(mixed, o_mixed)
        cm.wait()
        rows = x[...].astype(f32) + (mm(mixed[...], wm[...], 1, 0) + mb)
        after[...] = rows
        c.out(after, o_after)
        xhat, _ = norm_stats(rows)
        n2[...] = (xhat * g2 + s2).astype(bf)
        c.out(n2, o_n2)
        cu.wait()

        def block(j, carry):
            s = pl.ds(pl.multiple_of(j * 256, 256), 256)
            a, b = gelu_parts(mm(n2[...], wu[:, s], 1, 0) + ub[:, s])
            act[:, s] = a.astype(bf)
            slope[:, s] = b.astype(bf)
            return carry

        lax.fori_loop(0, FF // 256, block, 0)
        c.out(act, o_act)
        c.out(slope, o_slope)
        cd.wait()
        out[...] = (after[...] + (mm(act[...], wd[...], 1, 0) + db)).astype(bf)
        c.out(out, o_out)
        c.finish()


SAVED = (((L, D), bf), ((L, 3 * D), bf), ((16, L), f32), ((L, D), bf), ((L, D), f32), ((L, D), bf),
         ((L, FF), bf), ((L, FF), bf), ((L, D), bf))


def shapes(spec):
    return [jax.ShapeDtypeStruct(*one) for one in spec]


def scratch(spec):
    return [pltpu.VMEM(*one) for one in spec]


PARAMS = pltpu.CompilerParams(vmem_limit_bytes=62 << 20)


def forward(side, x, clip, vec, ub, weights, old=None):
    extra = 0 if old is None else 9
    xt = ((L, D), x.dtype)
    ws = [(w.shape, w.dtype) for w in weights]
    return pl.pallas_call(
        functools.partial(front, clip, extra),
        out_shape=shapes(SAVED),
        in_specs=[SM, ANY, VM, VM] + [ANY] * (4 + extra),
        out_specs=[ANY] * 9,
        scratch_shapes=scratch([xt] + ws + list(SAVED)) + [pltpu.SemaphoreType.DMA((20,))],
        input_output_aliases={8 + i: i for i in range(extra)},
        compiler_params=PARAMS,
        cost_estimate=pl.CostEstimate(flops=8_050_000_000, bytes_accessed=30_000_000, transcendentals=5_000_000),
    )(side, x, vec, ub, *weights, *(old or ()))


def mlp_back(clip, extra, side, g_in, vec, slope_in, after_in, wu_in, wd_in, *rest):
    o_gl, o_ga, o_gb, o_vec = rest[extra : extra + 4]
    g, slope, after, wu, wd, gl, ga, gb, vout, sems = rest[extra + 4 :]

    @pl.when(side[0] != 0)
    def _():
        c = Copies(sems)
        cg = c.start(g_in.at[clip] if clip is not None else g_in, g)
        tiles = [slice(j * D, (j + 1) * D) for j in range(FF // D)]

        def load(s):
            return c.start(wd_in.at[s], wd.at[s]), c.start(slope_in.at[:, s], slope.at[:, s])

        pairs = [load(s) for s in tiles]
        cu = c.start(wu_in, wu)
        ca = c.start(after_in, after)
        cg.wait()
        for j, s in enumerate(tiles):
            for copy in pairs[j]:
                copy.wait()
            piece = (mm(g[...], wd[s, :], 1, 1) * slope[:, s].astype(f32)).astype(bf)
            gl[:, s] = piece
            vout[0:1, s] = jnp.sum(piece.astype(f32), axis=0, keepdims=True)
        c.out(gl, o_gl)
        cu.wait()
        ca.wait()
        e = mm(gl[...], wu[...], 1, 1)
        xhat, rstd = norm_stats(after[...])
        gv = g[...].astype(f32)
        vout[1:2, 0:D] = jnp.sum(e * xhat, axis=0, keepdims=True)
        vout[1:2, D : 2 * D] = jnp.sum(e, axis=0, keepdims=True)
        vout[1:2, 2 * D : 3 * D] = jnp.sum(gv, axis=0, keepdims=True)
        whole = gv + norm_back(e, xhat, rstd, vec[5:6, :])
        ga[...] = whole
        gb[...] = whole.astype(bf)
        c.out(ga, o_ga)
        c.out(gb, o_gb)
        c.out(vout, o_vec)
        c.finish()


MB_OUT = (((L, FF), bf), ((L, D), f32), ((L, D), bf), ((8, FF), f32))


def backward_mlp(side, g, clip, vec, slope, after, wu, wd, old=None):
    extra = 0 if old is None else 4
    sc = [((L, D), bf), ((L, FF), bf), ((L, D), f32), (wu.shape, bf), (wd.shape, bf)]
    return pl.pallas_call(
        functools.partial(mlp_back, clip, extra),
        out_shape=shapes(MB_OUT),
        in_specs=[SM, ANY, VM] + [ANY] * (4 + extra),
        out_specs=[ANY] * 4,
        scratch_shapes=scratch(sc + list(MB_OUT)) + [pltpu.SemaphoreType.DMA((24,))],
        input_output_aliases={7 + i: i for i in range(extra)},
        compiler_params=PARAMS,
        cost_estimate=pl.CostEstimate(flops=4_830_000_000, bytes_accessed=20_000_000, transcendentals=1000),
    )(side, g, vec, slope, after, wu, wd, *(old or ()))


def attn_back(clip, lead, extra, side, ga_in, x_in, vec, flags, qkv_in, lt_in, wm_in, wj_in, *rest):
    o_gj, o_gh, o_vec = rest[extra : extra + 3]
    rest = rest[extra + 3 :]
    if lead:
        o_full, full, rest = rest[0], rest[-2], rest[1:-2] + rest[-1:]
    ga, x, qkv, lt, wm, wj, gm, gb, gj, gh, vout, sems = rest

    @pl.when(side[0] != 0)
    def _():
        c = Copies(sems)
        cg = c.start(ga_in, ga)
        cm = c.start(wm_in, wm)
        cq = c.start(qkv_in, qkv)
        cl = c.start(lt_in, lt)
        cg.wait()
        cm.wait()
        gb[...] = ga[...].astype(bf)
        gm[...] = mm(gb[...], wm[...], 1, 1).astype(bf)
        cq.wait()
        cl.wait()
        cj = c.start(wj_in, wj)
        cx = c.start(x_in.at[clip] if clip is not None else x_in, x)
        lane = lax.broadcasted_iota(jnp.int32, (L, 128), 1)

        def pair(p, carry):
            cols = [pl.ds(pl.multiple_of(p * 128 + part * D, 128), 128) for part in range(3)]
            q, k, v = [qkv[:, s] for s in cols]
            go = gm[:, cols[0]]
            res = []
            for h in range(2):
                own = (lane < 64) == (h == 0)
                km = jnp.where(own, k, jnp.zeros_like(k))
                vm = jnp.where(own, v, jnp.zeros_like(v))
                w = jnp.exp2(mm(km, q, 1, 1) * SCORE - lt[pl.ds(2 * p + h, 1), :])
                gw = mm(vm, go, 1, 1)
                inner = jnp.sum(w * gw, axis=0, keepdims=True)
                gs = (w * (gw - inner)).astype(bf)
                res.append((mm(gs, k, 0, 0), mm(gs, q, 1, 0), mm(w.astype(bf), go, 1, 0)))
            for part, scale in enumerate((HD ** (-0.5), HD ** (-0.5), 1.0)):
                both = jnp.where(lane < 64, res[0][part], res[1][part])
                gj[:, cols[part]] = (both * scale).astype(bf)
            return carry

        lax.fori_loop(0, HEADS // 2, pair, 0)
        c.out(gj, o_gj)
        cj.wait()
        cx.wait()
        e = mm(gj[...], wj[...], 1, 1)
        xhat, rstd = norm_stats(x[...].astype(f32))
        vout[0:1, :] = jnp.sum(e * xhat, axis=0, keepdims=True)
        vout[1:2, :] = jnp.sum(e, axis=0, keepdims=True)
        vout[2:3, :] = jnp.sum(gj[:, 0:D].astype(f32), axis=0, keepdims=True)
        vout[3:4, :] = jnp.sum(gj[:, 2 * D :].astype(f32), axis=0, keepdims=True)
        vout[4:5, :] = jnp.sum(gb[...].astype(f32), axis=0, keepdims=True)
        whole = ga[...] + norm_back(e, xhat, rstd, vec[0:1, :])
        if lead:
            free = whole * (1.0 - flags[clip].astype(f32))
            full[...] = whole
            c.out(full, o_full)
            vout[5:6, :] = jnp.sum(whole - free, axis=0, keepdims=True)
            whole = free
        gh[...] = whole.astype(bf)
        c.out(gh, o_gh)
        c.out(vout, o_vec)
        c.finish()


def backward_attn(side, ga, x, clip, vec, flags, qkv, lt, wm, wj, old=None):
    lead = old is not None
    extra = 3 if lead else 0
    outs = (((L, 3 * D), bf), ((L, D), bf), ((8, D), f32))
    full = (((L, D), f32),) if lead else ()
    sc = [((L, D), f32), ((L, D), x.dtype), ((L, 3 * D), bf), ((16, L), f32), (wm.shape, bf), (wj.shape, bf), ((L, D), bf), ((L, D), bf)]
    return pl.pallas_call(
        functools.partial(attn_back, clip, lead, extra),
        out_shape=shapes(outs + full),
        in_specs=[SM, ANY, ANY, VM, VM] + [ANY] * (4 + extra),
        out_specs=[ANY] * (3 + lead),
        scratch_shapes=scratch(sc + list(outs + full)) + [pltpu.SemaphoreType.DMA((16,))],
        input_output_aliases={9 + i: i for i in range(extra)},
        compiler_params=PARAMS,
        cost_estimate=pl.CostEstimate(flops=4_400_000_000, bytes_accessed=20_000_000, transcendentals=3_000_000),
    )(side, ga, x, vec, flags, qkv, lt, wm, wj, *(old or ()))


def weight_grad(a0, b0, a1, b1, o_ref, a, b, o, sems):
    c = Copies(sems)
    waits = [c.start(src, dst) for src, dst in ((a0, a.at[0:L]), (a1, a.at[L:]), (b0, b.at[0:L]), (b1, b.at[L:]))]
    for w in waits:
        w.wait()
    rows, cols = o.shape
    if rows > D:
        for j in range(rows // D):
            s = slice(j * D, (j + 1) * D)
            o[s, :] = mm(a[:, s], b[...], 0, 0).astype(bf)
            c.out(o.at[s], o_ref.at[s])
    else:
        for j in range(cols // D):
            s = slice(j * D, (j + 1) * D)
            o[:, s] = mm(a[...], b[:, s], 0, 0).astype(bf)
            c.out(o.at[:, s], o_ref.at[:, s])
    c.finish()


def weight_gradient(a0, b0, a1, b1):
    m, n = a0.shape[1], b0.shape[1]
    return pl.pallas_call(
        weight_grad,
        out_shape=jax.ShapeDtypeStruct((m, n), bf),
        in_specs=[ANY] * 4,
        out_specs=ANY,
        scratch_shapes=scratch([((2 * L, m), bf), ((2 * L, n), bf), ((m, n), bf)]) + [pltpu.SemaphoreType.DMA((16,))],
        compiler_params=PARAMS,
        cost_estimate=pl.CostEstimate(flops=4 * L * m * n, bytes_accessed=2 * (2 * L * (m + n) + m * n), transcendentals=0),
    )(a0, b0, a1, b1)


def passed_along(block, distance):
    devices = range(lax.axis_size("section"))
    route = [(i - distance, i) for i in devices if i - distance in devices]
    return lax.ppermute(block, "section", route)


def scatter(values):
    return lax.psum_scatter(values, "batch", scatter_dimension=0, tiled=True)


def split_grad(kind, count, part, *refs):
    ins, (keep, send), (a, b, o, sems) = refs[:-6], refs[-6:-4], refs[-4:]
    c = Copies(sems)
    mine = part[0]
    tiles = [slice(j * D, (j + 1) * D) for j in range(FF // D)]
    if kind == "down":
        a0, b0, a1, b1, other = ins
        rows = (b.at[0:L], b.at[L:])
        own = [pltpu.make_async_copy(src, dst, sems.at[30 + i]) for i, (src, dst) in enumerate(zip((b0, b1), rows))]

        @pl.when(part[1] != 0)
        def _():
            for copy in own:
                copy.start()

        @pl.when(part[1] == 0)
        def _():
            for at in range(2):
                pltpu.make_async_copy(other.at[at], rows[at], sems.at[30 + at]).start()

        def load(s):
            return c.start(a0.at[:, s], a.at[0:L, s]), c.start(a1.at[:, s], a.at[L:, s])

        loads = [load(s) for s in tiles[:2]]
        for copy in own:
            copy.wait()
        height = FF // count
        per = D // height // 2
        for j, s in enumerate(tiles):
            for copy in loads[j]:
                copy.wait()
            if j + 2 < len(tiles):
                loads.append(load(tiles[j + 2]))
            tile = mm(a[:, s], b[...], 0, 0).astype(bf)
            for i in range(2 * per):
                o[i % 2, j * per + i // 2] = tile[i * height : (i + 1) * height]
            s = slice(j * per, (j + 1) * per)
            c.out(o.at[mine, s], keep.at[s])
            c.out(o.at[1 - mine, s], send.at[s])
    else:
        height = D // count
        units = []
        for g, first in enumerate(range(0, len(ins), 4)):
            a0, b0, a1, b1 = ins[first : first + 4]
            l = slice(g * D, (g + 1) * D)
            moves = [(a0, a.at[0:L, l]), (a1, a.at[L:, l])]
            for s in tiles[: b0.shape[1] // D]:
                r = slice(len(units) * D, (len(units) + 1) * D)
                moves += [(b0.at[:, s], b.at[0:L, r]), (b1.at[:, s], b.at[L:, r])]
                units.append((l, r, moves))
                moves = []
        loads = [[c.start(*move) for move in unit[2]] for unit in units[:2]]
        for t, (l, r, _) in enumerate(units):
            for copy in loads[t]:
                copy.wait()
            if t + 2 < len(units):
                loads.append([c.start(*move) for move in units[t + 2][2]])
            tile = mm(a[:, l], b[:, r], 0, 0).astype(bf)
            s = slice(t * height, (t + 1) * height)
            for i in range(count):
                o[i % 2, i // 2, s] = tile[i * height : (i + 1) * height]
            c.out(o.at[mine, :, s], keep.at[:, s])
            c.out(o.at[1 - mine, :, s], send.at[:, s])
    c.finish()


def split_gradient(kind, count, part, groups):
    flat = [one for group in groups for one in group]
    m = sum(group[0].shape[1] for group in groups)
    n = sum(group[1].shape[1] for group in groups)
    area = sum(group[0].shape[1] * group[1].shape[1] for group in groups)
    half = jax.ShapeDtypeStruct((count // 2, area // D // count, D), bf)
    return pl.pallas_call(
        functools.partial(split_grad, kind, count),
        out_shape=(half, half),
        in_specs=[SM] + [ANY] * len(flat),
        out_specs=(ANY, ANY),
        scratch_shapes=scratch([((2 * L, m), bf), ((2 * L, n), bf), ((2,) + half.shape, bf)]) + [pltpu.SemaphoreType.DMA((32,))],
        compiler_params=PARAMS,
        cost_estimate=pl.CostEstimate(flops=4 * L * area, bytes_accessed=2 * (2 * L * (m + n) + area), transcendentals=0),
    )(part, *flat)


def swapped(values, bit):
    return lax.ppermute(values, "batch", [(i, i ^ bit) for i in range(lax.axis_size("batch"))])


def added(left, right):
    return left.astype(f32) + right.astype(f32)


def after(value, *others):
    return lax.optimization_barrier((value,) + others)


def halve(keep, send, place, level):
    came = swapped(send, 1 << level)
    if keep.shape[0] == 1:
        return added(keep[0], came[0])
    own = (place >> (level + 1)) & 1
    shape = (keep.shape[0] // 2, 2) + keep.shape[1:]
    kept, got = keep.reshape(shape), came.reshape(shape)

    def pick(side):
        return added(lax.dynamic_index_in_dim(kept, side, 1, False), lax.dynamic_index_in_dim(got, side, 1, False)).astype(bf)

    return pick(own), pick(1 - own)


def summed(values, place):
    levels = lax.axis_size("batch").bit_length() - 1
    split = min(levels, 3)

    def exchange(block, level):
        return swapped(block, 1 << level)

    for level in range(split):
        own = (place >> level) & 1
        parts = values.reshape(2, -1, D)
        came = exchange(lax.dynamic_index_in_dim(parts, 1 - own, 0, False), level)
        values = added(lax.dynamic_index_in_dim(parts, own, 0, False), came).astype(bf)
    for level in range(split, levels):
        values = added(values, exchange(values, level)).astype(bf)
    for level in reversed(range(split)):
        own = (place >> level) & 1
        came = exchange(values, level)
        low, high = jnp.where(own == 0, values, came), jnp.where(own == 0, came, values)
        values = jnp.concatenate([low, high])
    return values


def collect_small(flag, b0, b1, v0, v1, a0, a1, here, moved):
    half = L // 2
    for out, s in ((here, slice(0, half)), (moved, slice(half, L))):
        out[0:half, :] = (b0[s, :] + b1[s, :]).astype(bf)
        out[half:, :] = jnp.zeros((out.shape[0] - half, D), bf)
    vm = v0[...] + v1[...]
    va = a0[...] + a1[...]
    for out in (here, moved):
        out[half : half + 1, :] = va[5:6].astype(bf)
    block = jnp.concatenate([vm[0:1, i * D : (i + 1) * D] for i in range(4)] + [vm[1:2, i * D : (i + 1) * D] for i in range(3)]
                            + [va[i : i + 1] for i in range(5)] + [jnp.zeros((4, D), f32)])
    here[half + 16 : half + 32, :] = block.astype(bf)


def collect(*values):
    return pl.pallas_call(
        collect_small,
        out_shape=[jax.ShapeDtypeStruct((L // 2 + more, D), bf) for more in (128, 16)],
        in_specs=[SM] + [VM] * 6,
        out_specs=[VM, VM],
        cost_estimate=pl.CostEstimate(flops=1_000_000, bytes_accessed=5_000_000, transcendentals=0),
    )(*values)


def shards(clips, mask_flags, mask_embed, pos_embed, first_gain, first_shift, joint_weight, query_bias, value_bias,
           mixer_weight, mixer_bias, second_gain, second_shift, up_weight, up_bias, down_weight, down_bias, out_grad):
    first = lax.axis_index("section") == 0
    lead = first.astype(jnp.int32).reshape(1)
    tail = 1 - lead
    count = lax.axis_size("batch")
    keep = mask_flags.astype(f32)[..., None]
    blended = clips.astype(f32) * (1.0 - keep) + keep * mask_embed + pos_embed
    vec = jnp.concatenate([first_gain, first_shift, query_bias, value_bias, mixer_bias, second_gain, second_shift, down_bias])
    wj, wm, wu, wd = joint_weight[0], mixer_weight[0], up_weight[0], down_weight[0]
    weights = (wj, wm, wu, wd)

    flags = mask_flags[..., None]
    place = lax.axis_index("batch")
    part = jnp.stack([place % 2, lead[0]]).astype(jnp.int32)
    fast = (D // count) % 16 == 0

    lead0 = forward(lead, blended, 0, vec, up_bias, weights)
    arriving0 = passed_along(lead0[8], 1)
    lead1 = forward(lead, blended, 1, vec, up_bias, weights)
    arriving1 = passed_along(lead1[8], 1)

    def back(side, saved, g, x, clip, old):
        _, qkv, lt, _, after_rows, _, _, slope, _ = saved
        own = clip if old is None else None
        gl, ga, gb, vm = backward_mlp(side, g, own, vec, slope, after_rows, wu, wd, old and old[:4])
        at = None if old is None else clip
        gj, gh, va, *full = backward_attn(side, ga, x, at, vec, flags, qkv, lt, wm, wj, old and old[4:])
        return (gl, ga, gb, vm, gj, gh, va), full

    saved0 = forward(tail, arriving0, None, vec, up_bias, weights, lead0)
    grads0, _ = back(tail, saved0, out_grad, arriving0, 0, None)
    leaving0 = passed_along(grads0[5], -1)
    saved1 = forward(tail, arriving1, None, vec, up_bias, weights, lead1)
    grads1, _ = back(tail, saved1, out_grad, arriving1, 1, None)
    leaving1 = passed_along(grads1[5], -1)
    grads0, (blend0,) = back(lead, saved0, leaving0, blended, 0, grads0)
    va0 = grads0[6]

    n1_1, qkv_1, lt_1, mixed_1, after_1, n2_1, act_1, slope_1, _ = saved1
    if fast:
        part_d, va0 = after(part, va0)
        down = split_gradient("down", count, part_d, [(saved0[6], leaving0, act_1, leaving1, out_grad)])
        lead_m, *down = after(lead, *down)
        gl1, ga1, gb1, vm1 = backward_mlp(lead_m, leaving1, None, vec, slope_1, after_1, wu, wd, grads1[:4])
        down = halve(*down, place, 0)
        part_u, *down = after(part, *down)
        up = split_gradient("up", count, part_u, [(saved0[5], grads0[0], n2_1, gl1), (saved0[3], grads0[2], mixed_1, gb1)])
        up = halve(*up, place, 0)
        lead_a, *up = after(lead, *up)
    else:
        gl1, ga1, gb1, vm1 = backward_mlp(lead, leaving1, None, vec, slope_1, after_1, wu, wd, grads1[:4])
        lead_a = lead
    gj1, gh1, va1, blend1 = backward_attn(lead_a, ga1, blended, 1, vec, flags, qkv_1, lt_1, wm, wj, grads1[4:])
    here, moved = collect(lead, blend0, blend1, grads0[3], vm1, va0, va1)
    joint_group, mixer_group = (saved0[0], grads0[4], n1_1, gj1), (saved0[3], grads0[2], mixed_1, gb1)
    if fast:
        down = halve(*down, place, 1)
        part_b, *down = after(part, *down)
        joint = split_gradient("joint", count, part_b, [joint_group])
        levels = count.bit_length() - 1
        down, up, joint = [functools.reduce(lambda pair, level: halve(*pair, place, level), range(at, levels), value)
                           for at, value in ((2, down), (1, up), (0, joint))]
        height = D // count

        def wide(block):
            return jnp.swapaxes(block.reshape(-1, height, D), 0, 1).reshape(height, -1)

        up, joint, mixer = wide(up[: 4 * height]), wide(joint), up[4 * height :]
    else:
        g0 = jnp.where(first, leaving0, out_grad[0])
        g1 = jnp.where(first, leaving1, out_grad[1])
        down_group, up_group = (saved0[6], g0, act_1, g1), (saved0[5], grads0[0], n2_1, gl1)
        down, up, joint, mixer = [
            scatter(weight_gradient(*group)).astype(f32) for group in (down_group, up_group, joint_group, mixer_group)
        ]
    down, up, joint, mixer = [one[None] for one in (down, up, joint, mixer)]

    layer_outputs = jnp.stack([saved0[8], saved1[8]])[None]
    input_grads = jnp.stack([grads0[5], gh1])[None]
    half = L // 2
    arrived = passed_along(moved, 1)
    top = jnp.where(first, here[: half + 16], arrived)
    total = summed(jnp.concatenate([top, here[half + 16 :]]), place).astype(f32)
    grad_position = total[:half]
    grad_mask = lax.dynamic_slice(total[half], (jnp.where(first, 0, D // 2),), (D // 2,))
    sums = total[half + 16 :]
    g_ub = lax.dynamic_slice(sums[:4].reshape(1, FF), (0, place * (FF // count)), (1, FF // count))
    rest = lax.dynamic_slice(sums[4:12], (0, place * (D // count)), (8, D // count))
    g_gain2, g_shift2, g_db, g_gain1, g_shift1, g_qb, g_vb, g_mb = [rest[i : i + 1] for i in range(8)]
    return (layer_outputs, input_grads, g_gain1, g_shift1, joint, g_qb, g_vb, mixer, g_mb, g_gain2, g_shift2, up, g_ub,
            down, g_db, grad_mask, grad_position)


def solution(mesh):
    whole, section, both = P(), P("section"), P("section", "batch")
    in_specs = (P("batch"), P("batch"), whole, whole) + (section,) * 13 + (P("batch"),)
    out_specs = (both,) * 15 + (section, section)

    def step(*arrays):
        return shards(*arrays)

    step = jax.shard_map(step, mesh=mesh, in_specs=in_specs, out_specs=out_specs, check_vma=False)
    return step
```
